256 devices in a mesh: group: 4 (over y_hi, core), member: 64 (over z, y_lo, x).
Axes of the slice: x: 4, y: 4 (y_hi: 2, y_lo: 2; y = y_hi * 2 + y_lo), z: 8, core: 2. Of those that a mesh axis runs over, the one named last changes fastest.
Arguments:
- coefficients: float32 [2048, 3, 289], P(('group', 'member')), may hold values from -2.5 to 2.5
- pair_list: int32 [4096, 2], P(('group', 'member')), may hold values from -1 to 2047, as said below
- pair_offset: float32 [4096, 3], P(('group', 'member')), may hold values from -2.6 to 2.6
Outputs:
- force_coef: float32 [2048, 3, 289], P(('group', 'member'))
The draws below stay inside these ranges and needn't reach their ends.
Inputs may be any that keep to these rules, and one draw needn't show every extreme that they name: `pair_list`: each row is (i, j) or (-1, -1) for an empty slot; on every device the live rows come first and some device has all 16 rows live. i is owned by a device of the pair owner's group; j is too, or else j is one of the first 4 vesicles of the device with the same member index in an adjacent group. Of one device's in-group entries (i and j), at most 2 are owned by any one device, and the full device reaches 2.
All inputs are finite; a program needn't handle non-finite values.
Results may differ from the reference program's by a relative error of at most 0.0003.
Values sent between devices are 32-bit elements; how exact they have to be, the bound alone decides.
No kernel may reach another device: no remote copies, remote signals or barrier semaphores. Data moves between devices by JAX's collectives and lax.ppermute only.
A program may use at most 64 MiB of HBM per device.

```python
import math
import jax
import jax.numpy as jnp
from jax import lax

ORDER = 16
UPORDER = 32
NCOEF = 289
VES_DEV = 8
PAIR_DEV = 16
RIM_VES = 4
CAP = 2
VESICLES = 2048
PAIRS = 4096
N_GROUP = 4
N_MEMBER = 64
DEVICES = 256


def draw_coefficients(key, part):
    rough_key = jax.random.fold_in(key, 0)
    coef_index = jnp.arange(NCOEF)[None, :]
    component = jnp.arange(3)[:, None]
    sphere = math.sqrt(4.0 * math.pi / 3.0)
    sphere_part = jnp.where((component == 0) & (coef_index == 3), -sphere, 0.0)
    sphere_part = sphere_part + jnp.where((component == 1) & (coef_index == 1), -sphere, 0.0)
    sphere_part = sphere_part + jnp.where((component == 2) & (coef_index == 2), sphere, 0.0)
    rough_part = jnp.clip(jax.random.normal(rough_key, (VESICLES, 3, NCOEF), jnp.float32), -4.0, 4.0) * 0.06
    return (sphere_part[None, :, :].astype(jnp.float32) + rough_part).astype(jnp.float32)


def draw_pair_offset(key, part):
    height_key, turn_key, gap_key = jax.random.split(key, 3)
    height = jax.random.uniform(height_key, (PAIRS,), jnp.float32, -1.0, 1.0)
    turn = jax.random.uniform(turn_key, (PAIRS,), jnp.float32, -math.pi, math.pi)
    gap = jax.random.uniform(gap_key, (PAIRS,), jnp.float32, 0.05, 0.25)
    cycle = jnp.sqrt(jnp.maximum(1.0 - height * height, 0.0))
    reach = 2.0 + gap
    direction = jnp.stack([cycle * jnp.cos(turn), cycle * jnp.sin(turn), height], axis=-1)
    return (direction * reach[:, None]).astype(jnp.float32)


def draw_pair_list(key, part):
    key_list = jax.random.split(key, 8)
    device = jnp.arange(DEVICES)
    group_of = device // N_MEMBER
    member_of = device % N_MEMBER
    live_count = jax.random.randint(key_list[0], (DEVICES,), PAIR_DEV - PAIR_DEV // 4, PAIR_DEV + 1)
    full_device = jax.random.randint(key_list[1], (), 0, DEVICES)
    live_count = jnp.where(device == full_device, PAIR_DEV, live_count)
    owners_used = 2 * PAIR_DEV // CAP
    owner_order = jax.vmap(lambda sub_key: jax.random.permutation(sub_key, N_MEMBER))(jax.random.split(key_list[2], DEVICES))
    end_order = jax.vmap(lambda sub_key: jax.random.permutation(sub_key, 2 * PAIR_DEV))(jax.random.split(key_list[3], DEVICES))
    owner_pick = end_order % owners_used
    owner_member = jnp.take_along_axis(owner_order, owner_pick, axis=1)
    local_pick = jax.random.randint(key_list[4], (DEVICES, 2 * PAIR_DEV), 0, VES_DEV)
    inside_id = (group_of[:, None] * N_MEMBER + owner_member) * VES_DEV + local_pick
    ghost_flag = (jax.random.randint(key_list[5], (DEVICES, PAIR_DEV), 0, 16) == 0) & (owner_pick[:, 1::2] != 0)
    upward = jax.random.randint(key_list[6], (DEVICES, PAIR_DEV), 0, 2) * 2 - 1
    other_group = group_of[:, None] + upward
    other_group = jnp.where(other_group < 0, group_of[:, None] + 1, jnp.where(other_group >= N_GROUP, group_of[:, None] - 1, other_group))
    rim_pick = jax.random.randint(key_list[7], (DEVICES, PAIR_DEV), 0, RIM_VES)
    ghost_id = (other_group * N_MEMBER + member_of[:, None]) * VES_DEV + rim_pick
    first_ids = inside_id[:, 0::2]
    second_ids = jnp.where(ghost_flag, ghost_id, inside_id[:, 1::2])
    live_flag = jnp.arange(PAIR_DEV)[None, :] < live_count[:, None]
    first_ids = jnp.where(live_flag, first_ids, -1)
    second_ids = jnp.where(live_flag, second_ids, -1)
    return jnp.stack([first_ids, second_ids], axis=-1).reshape(PAIRS, 2).astype(jnp.int32)


def setup_inputs(seed: int = 0) -> dict:
    arg_keys = jax.random.split(jax.random.key(seed), 4)
    coefficients = draw_coefficients(jax.random.fold_in(arg_keys[3], 71), 0)
    pair_list = draw_pair_list(jax.random.fold_in(arg_keys[3], 71), 0)
    pair_offset = draw_pair_offset(jax.random.fold_in(arg_keys[3], 71), 0)
    return {"coefficients": coefficients, "pair_list": pair_list, "pair_offset": pair_offset}


def contact_width(up_order):
    return (0.7 * math.pi / (up_order + 1)) ** 2

def legendre_table(order_max, cosine, sine_theta):
    legendre = {}
    diagonal = jnp.ones_like(cosine) * math.sqrt(1.0 / (4.0 * math.pi))
    for azimuth in range(order_max + 1):
        if azimuth > 0:
            diagonal = -math.sqrt((2.0 * azimuth + 1.0) / (2.0 * azimuth)) * sine_theta * diagonal
        legendre[azimuth, azimuth] = diagonal
        if azimuth < order_max:
            legendre[azimuth + 1, azimuth] = math.sqrt(2.0 * azimuth + 3.0) * cosine * diagonal
        for degree in range(azimuth + 2, order_max + 1):
            factor_one = math.sqrt((4.0 * degree * degree - 1.0) / (degree * degree - azimuth * azimuth))
            factor_two = math.sqrt(((degree - 1.0) ** 2 - azimuth * azimuth) / (4.0 * (degree - 1.0) ** 2 - 1.0))
            legendre[degree, azimuth] = factor_one * (cosine * legendre[degree - 1, azimuth] - factor_two * legendre[degree - 2, azimuth])
    return legendre

def basis_table(order_max, up_order):
    lat_count = up_order + 1
    lon_count = 2 * up_order
    polar_angle = (jnp.arange(lat_count, dtype=jnp.float32) + 0.5) * (math.pi / lat_count)
    longitude = jnp.arange(lon_count, dtype=jnp.float32) * (2.0 * math.pi / lon_count)
    cosine = jnp.cos(polar_angle)
    sine_theta = jnp.sin(polar_angle)
    legendre = legendre_table(order_max, cosine, sine_theta)
    ones_row = jnp.ones_like(longitude)
    basis_rows = []
    for degree in range(order_max + 1):
        for azimuth in range(-degree, degree + 1):
            if azimuth == 0:
                beside_all = ones_row
            elif azimuth > 0:
                beside_all = math.sqrt(2.0) * jnp.cos(azimuth * longitude)
            else:
                beside_all = math.sqrt(2.0) * jnp.sin(-azimuth * longitude)
            basis_rows.append((legendre[degree, abs(azimuth)][:, None] * beside_all[None, :]).reshape(-1))
    harmonics = jnp.stack(basis_rows)
    weights = (sine_theta[:, None] * ones_row[None, :]).reshape(-1) * (math.pi / lat_count) * (2.0 * math.pi / lon_count)
    return (harmonics, weights)

def upsample(coef_block, harmonics):
    vesicle_count = coef_block.shape[0]
    surface = jnp.dot(coef_block.reshape(vesicle_count * 3, -1), harmonics, precision=lax.Precision.HIGHEST, preferred_element_type=jnp.float32)
    return surface.reshape(vesicle_count, 3, -1)

def project(point_force, harmonics, weights):
    vesicle_count = point_force.shape[0]
    weighted = (point_force * weights[None, None, :]).reshape(vesicle_count * 3, -1)
    result = jnp.dot(weighted, harmonics.T, precision=lax.Precision.HIGHEST, preferred_element_type=jnp.float32)
    return result.reshape(vesicle_count, 3, -1)

def pair_forces(near_side, far_side, width):
    factor = 1.0 / (near_side.shape[1] * width * width)
    delta_x = near_side[0][:, None] - far_side[0][None, :]
    delta_y = near_side[1][:, None] - far_side[1][None, :]
    delta_z = near_side[2][:, None] - far_side[2][None, :]
    dist_sq = delta_x * delta_x + delta_y * delta_y + delta_z * delta_z
    kernel = 1.0 / (1.0 + dist_sq / width)
    kernel = kernel * kernel
    on_near = jnp.stack([lax.optimization_barrier(jnp.sum(kernel * delta_x, axis=1)), lax.optimization_barrier(jnp.sum(kernel * delta_y, axis=1)), lax.optimization_barrier(jnp.sum(kernel * delta_z, axis=1))]) * factor
    on_far = -jnp.stack([lax.optimization_barrier(jnp.sum(kernel * delta_x, axis=0)), lax.optimization_barrier(jnp.sum(kernel * delta_y, axis=0)), lax.optimization_barrier(jnp.sum(kernel * delta_z, axis=0))]) * factor
    return (on_near, on_far)

def reference(coefficients, pair_list, pair_offset):
    harmonics, weights = basis_table(ORDER, UPORDER)
    width = contact_width(UPORDER)
    surfaces = upsample(coefficients, harmonics)

    def add_pair(point_force, pair_data):
        pair_ids, offset_row = pair_data
        first_id = jnp.maximum(pair_ids[0], 0).astype(jnp.int32)
        second_id = jnp.maximum(pair_ids[1], 0).astype(jnp.int32)
        near_side = lax.dynamic_index_in_dim(surfaces, first_id, 0, keepdims=False) + offset_row[:, None]
        far_side = lax.dynamic_index_in_dim(surfaces, second_id, 0, keepdims=False)

        def live_branch(unused):
            return pair_forces(near_side, far_side, width)

        def dead_branch(unused):
            return (jnp.zeros_like(near_side), jnp.zeros_like(near_side))
        on_near, on_far = lax.cond(pair_ids[0] >= 0, live_branch, dead_branch, 0)
        point_force = point_force.at[first_id].add(on_near)
        point_force = point_force.at[second_id].add(on_far)
        return (point_force, None)
    point_force, unused = lax.scan(add_pair, jnp.zeros_like(surfaces), (pair_list, pair_offset))
    return project(point_force, harmonics, weights)
```

```python
import functools
import math

import jax
import jax.numpy as jnp
import numpy as np
from jax import lax
from jax.experimental import pallas as pl
from jax.experimental.pallas import tpu as pltpu
from jax.sharding import PartitionSpec as P

ORDER = 16
UPORDER = 32
RIM_VES = 4
LATS = UPORDER + 1
LONS = 2 * UPORDER
POINTS = LATS * LONS
NCOEF = (ORDER + 1) ** 2
LANES = 128
TILES = -(-POINTS // LANES)
PADDED = TILES * LANES
WIDTH = (0.7 * math.pi / LATS) ** 2
SCALE = 1.0 / math.sqrt(WIDTH)
FACTOR = math.sqrt(WIDTH) / (POINTS * WIDTH * WIDTH)
FAR_AWAY = 1e15
F32 = jnp.float32
HIGHEST = lax.Precision.HIGHEST


def factor_tables():
    theta = (np.arange(LATS) + 0.5) * (math.pi / LATS)
    phi = np.arange(LONS) * (2.0 * math.pi / LONS)
    cosine, sine = np.cos(theta), np.sin(theta)
    legendre = {}
    diagonal = np.full_like(cosine, math.sqrt(1.0 / (4.0 * math.pi)))
    for m in range(ORDER + 1):
        if m > 0:
            diagonal = -math.sqrt((2.0 * m + 1.0) / (2.0 * m)) * sine * diagonal
        legendre[m, m] = diagonal
        if m < ORDER:
            legendre[m + 1, m] = math.sqrt(2.0 * m + 3.0) * cosine * diagonal
        for l in range(m + 2, ORDER + 1):
            one = math.sqrt((4.0 * l * l - 1.0) / (l * l - m * m))
            two = math.sqrt(((l - 1.0) ** 2 - m * m) / (4.0 * (l - 1.0) ** 2 - 1.0))
            legendre[l, m] = one * (cosine * legendre[l - 1, m] - two * legendre[l - 2, m])
    lat = np.zeros((3 * LANES, LANES))
    lon = np.zeros((3 * LANES, LANES))
    row = 0
    for l in range(ORDER + 1):
        for m in range(-l, l + 1):
            lat[row, :LATS] = legendre[l, abs(m)]
            if m == 0:
                wave = np.ones(LONS)
            elif m > 0:
                wave = math.sqrt(2.0) * np.cos(m * phi)
            else:
                wave = math.sqrt(2.0) * np.sin(-m * phi)
            lon[row, :LONS] = wave
            lon[row, LONS:] = wave
            row += 1
    weights = np.zeros((8, PADDED))
    weights[:, :POINTS] = np.repeat(sine * (math.pi / LATS) * (2.0 * math.pi / LONS), LONS) * FACTOR
    return lat.astype(np.float32), lon.astype(np.float32), weights.astype(np.float32)


def pick_kernel(asked_ref, tiles_ref, out_ref):
    def pick(slot, carry):
        source = jnp.maximum(asked_ref[slot], 0)
        out_ref[slot] = tiles_ref[source]
        return carry

    lax.fori_loop(0, out_ref.shape[0], pick, 0, unroll=8)


def pair_kernel(
    slots,
    rows,
    meta_ref,
    offset_ref,
    lat_ref,
    lon_ref,
    weight_ref,
    received_ref,
    low_ref,
    high_ref,
    slot_out,
    low_out,
    high_out,
    source,
    ends,
    basis,
    surface,
    turned,
    force,
    near_turned,
    far_wide,
    far_sum,
    near_wide,
    near_sum,
):
    pairs = meta_ref.shape[0] // 2
    sub = rows // 8
    blocks = POINTS // rows
    count = slots.total
    live = meta_ref[2 * pairs]
    rims = low_ref.shape[0] // 8

    source[: count * 8] = received_ref[...]
    source[count * 8 : (count + rims) * 8] = low_ref[...]
    source[(count + rims) * 8 :] = high_ref[...]
    for pair in range(pairs):
        for side in range(2):
            start = pl.multiple_of(meta_ref[side * pairs + pair] * 8, 8)
            ends[(side * pairs + pair) * 8 : (side * pairs + pair + 1) * 8] = source[pl.ds(start, 8)]

    def chunk(index):
        return ends[pl.ds(index, 2 * pairs, stride=8), :]

    tails = chunk(6)
    tail_rows = [tails, pltpu.roll(tails, LANES // 2, 1), chunk(7)]
    coefs = jnp.concatenate(
        [
            jnp.concatenate([chunk(2 * c), chunk(2 * c + 1), tail_rows[c]], axis=1)
            for c in range(3)
        ],
        axis=0,
    )
    shift = offset_ref[...] * SCALE
    lane = lax.broadcasted_iota(jnp.int32, (8, LANES), 1)
    half = lax.broadcasted_iota(jnp.int32, lat_ref.shape, 1) < LONS
    for t in range(TILES):
        lanes = slice(t * LANES, (t + 1) * LANES)
        lat = jnp.where(half, lat_ref[:, 2 * t : 2 * t + 1], lat_ref[:, 2 * t + 1 : 2 * t + 2])
        table = lat * lon_ref[...]
        basis[:, lanes] = table
        part = jnp.dot(coefs, table, precision=HIGHEST, preferred_element_type=F32)
        part = part * SCALE + shift
        if t == TILES - 1:
            valid = lax.broadcasted_iota(jnp.int32, part.shape, 1) < POINTS - t * LANES
            part = jnp.where(valid, part, FAR_AWAY)
        surface[:, lanes] = part
        near = jnp.concatenate(
            [part[c * 2 * pairs : c * 2 * pairs + pairs] for c in range(3)]
            + [jnp.zeros((LANES - 3 * pairs, LANES), F32)],
            axis=0,
        )
        turned[lanes, :] = near.T
    near_turned[...] = jnp.zeros_like(near_turned)
    force[...] = jnp.zeros_like(force)

    lane_wide = lax.broadcasted_iota(jnp.int32, (rows, LANES), 1)

    def spread(pair, block):
        start = pl.multiple_of(block * rows, 8)
        columns = pltpu.roll(turned[pl.ds(start, rows), :], lax.rem(LANES - pair, LANES), 1)
        for c in range(3):
            column = columns[:, c * pairs : c * pairs + 1]
            near_wide[c] = jnp.broadcast_to(column, (rows, LANES)).reshape(sub, 8, LANES)

    def gather_near(pair, block):
        start = pl.multiple_of(block * rows, 8)
        value = near_turned[pl.ds(start, rows), :]
        for c in range(3):
            total = jnp.sum(near_sum[c].reshape(rows, LANES), axis=1, keepdims=True)
            value = jnp.where(lane_wide == c * pairs + pair, total, value)
        near_turned[pl.ds(start, rows), :] = value

    def one_pair(pair, carry):
        for c in range(3):
            row = surface[pl.ds(c * 2 * pairs + pairs + pair, 1), :]
            far_wide[c] = jnp.broadcast_to(row, (8, PADDED))
        far_sum[...] = jnp.zeros_like(far_sum)
        near_sum[...] = jnp.zeros_like(near_sum)
        spread(pair, 0)

        def one_block(block, inner):
            near = [near_wide[c] for c in range(3)]
            gather_near(pair, jnp.maximum(block - 1, 0))
            spread(pair, jnp.minimum(block + 1, blocks - 1))
            near_acc = [jnp.zeros((sub, 8, LANES), F32) for _ in range(3)]
            for t in range(TILES):
                lanes = slice(t * LANES, (t + 1) * LANES)
                delta = [near[c] - far_wide[c, :, lanes][None] for c in range(3)]
                grown = (delta[0] * delta[0] + delta[1] * delta[1]) + (delta[2] * delta[2] + 1.0)
                kernel = 1.0 / grown
                kernel = kernel * kernel
                for c in range(3):
                    pull = kernel * delta[c]
                    near_acc[c] = near_acc[c] + pull
                    far_sum[c, :, lanes] = far_sum[c, :, lanes] + jnp.sum(pull, axis=0)
            for c in range(3):
                near_sum[c] = near_acc[c]
            return inner

        lax.fori_loop(0, blocks, one_block, 0)
        gather_near(pair, blocks - 1)
        for c in range(3):
            force[pl.ds(c * 2 * pairs + pairs + pair, 1), :] = -jnp.sum(
                far_sum[c], axis=0, keepdims=True
            )
        return carry

    lax.fori_loop(0, live, one_pair, 0)

    total = jnp.zeros((6 * pairs, 3 * LANES), F32)
    for t in range(TILES):
        lanes = slice(t * LANES, (t + 1) * LANES)
        near = near_turned[lanes, :].T
        for c in range(3):
            force[c * 2 * pairs : c * 2 * pairs + pairs, lanes] = near[c * pairs : (c + 1) * pairs]
        part = force[:, lanes] * weight_ref[0:1, lanes]
        total = total + lax.dot_general(
            part,
            basis[:, lanes],
            (((1,), (1,)), ((), ())),
            precision=HIGHEST,
            preferred_element_type=F32,
        )
    for c in range(3):
        block = total[c * 2 * pairs : (c + 1) * 2 * pairs]
        ends[pl.ds(2 * c, 2 * pairs, stride=8), :] = block[:, :LANES]
        ends[pl.ds(2 * c + 1, 2 * pairs, stride=8), :] = block[:, LANES : 2 * LANES]
    tail = [total[c * 2 * pairs : (c + 1) * 2 * pairs, 2 * LANES :] for c in range(3)]
    ends[pl.ds(6, 2 * pairs, stride=8), :] = tail[0] + pltpu.roll(tail[1], LANES // 2, 1)
    ends[pl.ds(7, 2 * pairs, stride=8), :] = tail[2]

    source[...] = jnp.zeros_like(source)

    def hand_out(pair, carry):
        for side in range(2):
            value = ends[pl.ds(pl.multiple_of((side * pairs + pair) * 8, 8), 8), :]
            start = pl.multiple_of(meta_ref[side * pairs + pair] * 8, 8)
            source[pl.ds(start, 8), :] = source[pl.ds(start, 8), :] + value
        return carry

    lax.fori_loop(0, live, hand_out, 0)
    slot_out[...] = source[: count * 8]
    low_out[...] = source[count * 8 : (count + rims) * 8]
    high_out[...] = source[(count + rims) * 8 :]


def collect_kernel(asked_ref, returned_ref, low_ref, high_ref, out_ref, total):
    vesicles = out_ref.shape[0]
    total[...] = jnp.zeros_like(total)
    rims = low_ref.shape[0]
    total[:rims] = low_ref[...] + high_ref[...]

    def add(slot, carry):
        asked = asked_ref[slot]
        row = jnp.where(asked >= 0, asked, vesicles)
        total[row] = total[row] + returned_ref[slot]
        return carry

    lax.fori_loop(0, returned_ref.shape[0], add, 0, unroll=4)
    rest = NCOEF - 2 * LANES
    for v in range(vesicles):
        for c in range(3):
            out_ref[v, c : c + 1, :LANES] = total[v, 2 * c : 2 * c + 1, :]
            out_ref[v, c : c + 1, LANES : 2 * LANES] = total[v, 2 * c + 1 : 2 * c + 2, :]
        out_ref[v, 0:1, 2 * LANES :] = total[v, 6:7, :rest]
        moved = pltpu.roll(total[v], LANES // 2, 1)
        out_ref[v, 1:2, 2 * LANES :] = moved[6:7, :rest]
        out_ref[v, 2:3, 2 * LANES :] = total[v, 7:8, :rest]


class Slots:
    def __init__(self, members, cap):
        self.members = members
        self.cap = cap
        self.total = members * cap

    def __repr__(self):
        return "slots"


def vmem():
    return pl.BlockSpec(memory_space=pltpu.VMEM)


def smem():
    return pl.BlockSpec(memory_space=pltpu.SMEM)


def per_device(coefficients, pair_list, pair_offset):
    members = lax.axis_size("member")
    groups = lax.axis_size("group")
    group_here = lax.axis_index("group")
    vesicles = coefficients.shape[0]
    pairs = pair_list.shape[0]
    slots = Slots(members, max(2, (2 * pairs + members - 1) // members))
    total_slots = slots.total
    forward = [(i, i + 1) for i in range(groups - 1)]
    backward = [(i + 1, i) for i in range(groups - 1)]

    end_ids = pair_list.T.reshape(-1)
    end_live = end_ids >= 0
    safe_ids = jnp.maximum(end_ids, 0)
    owner_device = safe_ids // vesicles
    owner_group = owner_device // members
    owner_member = owner_device % members
    owner_slot = safe_ids % vesicles
    inside = end_live & (owner_group == group_here)
    key = jnp.where(inside, owner_member, -1)
    order = jnp.arange(2 * pairs)
    same = (key[:, None] == key[None, :]) & (order[None, :] < order[:, None])
    earlier = jnp.sum(same.astype(jnp.int32), axis=1)
    end_slot = jnp.where(inside, owner_member * slots.cap + earlier, -1)
    hit = end_slot[None, :] == jnp.arange(total_slots)[:, None]
    request = jnp.max(jnp.where(hit, owner_slot[None, :], -1), axis=1)
    asked_for = lax.all_to_all(
        request.reshape(members, slots.cap), "member", split_axis=0, concat_axis=0, tiled=True
    ).reshape(-1)

    head = coefficients[:, :, : 2 * LANES].reshape(vesicles, 6, LANES)
    tail = jnp.pad(coefficients[:, :, 2 * LANES :], ((0, 0), (0, 1), (0, LANES // 2 - (NCOEF - 2 * LANES))))
    tiles = jnp.concatenate([head, tail.reshape(vesicles, 2, LANES)], axis=1)
    rim = tiles[:RIM_VES]
    low = lax.ppermute(rim, "group", forward)
    high = lax.ppermute(rim, "group", backward)

    outgoing = pl.pallas_call(
        pick_kernel,
        out_shape=jax.ShapeDtypeStruct((total_slots, 8, LANES), F32),
        in_specs=[smem(), vmem()],
        out_specs=vmem(),
        name="pick",
    )(asked_for, tiles)
    received = lax.all_to_all(
        outgoing.reshape(members, slots.cap, 8, LANES),
        "member",
        split_axis=0,
        concat_axis=0,
        tiled=True,
    )

    rim_row = (
        total_slots
        + jnp.where(owner_group < group_here, 0, RIM_VES)
        + jnp.minimum(owner_slot, RIM_VES - 1)
    )
    end_row = jnp.where(inside, end_slot, jnp.where(end_live, rim_row, 0))
    live_pairs = jnp.sum((pair_list[:, 0] >= 0).astype(jnp.int32))
    meta = jnp.concatenate([end_row, live_pairs[None]]).astype(jnp.int32)
    offsets = jnp.pad(pair_offset.T, ((0, 0), (0, pairs))).reshape(-1, 1)

    lat, lon, weights = factor_tables()
    rows = 96
    slot_force, low_force, high_force = pl.pallas_call(
        functools.partial(pair_kernel, slots, rows),
        out_shape=(
            jax.ShapeDtypeStruct((total_slots * 8, LANES), F32),
            jax.ShapeDtypeStruct((RIM_VES * 8, LANES), F32),
            jax.ShapeDtypeStruct((RIM_VES * 8, LANES), F32),
        ),
        in_specs=[smem()] + [vmem()] * 7,
        out_specs=(vmem(),) * 3,
        scratch_shapes=[
            pltpu.VMEM(((total_slots + 2 * RIM_VES) * 8, LANES), F32),
            pltpu.VMEM((2 * pairs * 8, LANES), F32),
            pltpu.VMEM((3 * LANES, PADDED), F32),
            pltpu.VMEM((6 * pairs, PADDED), F32),
            pltpu.VMEM((PADDED, LANES), F32),
            pltpu.VMEM((6 * pairs, PADDED), F32),
            pltpu.VMEM((PADDED, LANES), F32),
            pltpu.VMEM((3, 8, PADDED), F32),
            pltpu.VMEM((3, 8, PADDED), F32),
            pltpu.VMEM((3, rows // 8, 8, LANES), F32),
            pltpu.VMEM((3, rows // 8, 8, LANES), F32),
        ],
        compiler_params=pltpu.CompilerParams(vmem_limit_bytes=48 << 20),
        name="pair_forces",
    )(
        meta,
        offsets,
        jnp.asarray(lat),
        jnp.asarray(lon),
        jnp.asarray(weights),
        received.reshape(total_slots * 8, LANES),
        low.reshape(RIM_VES * 8, LANES),
        high.reshape(RIM_VES * 8, LANES),
    )
    returned = lax.all_to_all(
        slot_force.reshape(members, slots.cap, 8, LANES),
        "member",
        split_axis=0,
        concat_axis=0,
        tiled=True,
    )
    from_low = lax.ppermute(high_force.reshape(RIM_VES, 8, LANES), "group", forward)
    from_high = lax.ppermute(low_force.reshape(RIM_VES, 8, LANES), "group", backward)
    return pl.pallas_call(
        collect_kernel,
        out_shape=jax.ShapeDtypeStruct(coefficients.shape, F32),
        in_specs=[smem()] + [vmem()] * 3,
        out_specs=vmem(),
        scratch_shapes=[pltpu.VMEM((vesicles + 1, 8, LANES), F32)],
        name="collect",
    )(asked_for, returned.reshape(total_slots, 8, LANES), from_low, from_high)


def solution(mesh):
    return jax.shard_map(
        per_device,
        mesh=mesh,
        in_specs=(
            P(("group", "member"), None, None),
            P(("group", "member"), None),
            P(("group", "member"), None),
        ),
        out_specs=P(("group", "member"), None, None),
        check_vma=False,
    )
```

```python
import functools
import math

import jax
import jax.numpy as jnp
import numpy as np
from jax import lax
from jax.experimental import pallas as pl
from jax.experimental.pallas import tpu as pltpu
from jax.sharding import PartitionSpec as P

ORDER = 16
UPORDER = 32
RIM_VES = 4
LATS = UPORDER + 1
LONS = 2 * UPORDER
POINTS = LATS * LONS
NCOEF = (ORDER + 1) ** 2
LANES = 128
TILES = -(-POINTS // LANES)
PADDED = TILES * LANES
WIDTH = (0.7 * math.pi / LATS) ** 2
SCALE = 1.0 / math.sqrt(WIDTH)
FACTOR = math.sqrt(WIDTH) / (POINTS * WIDTH * WIDTH)
FAR_AWAY = 1e18
F32 = jnp.float32
BF16 = jnp.bfloat16
FEATURES = 64
SMALL = 16
COORDS = 48
HIGHEST = lax.Precision.HIGHEST


def factor_tables():
    theta = (np.arange(LATS) + 0.5) * (math.pi / LATS)
    phi = np.arange(LONS) * (2.0 * math.pi / LONS)
    cosine, sine = np.cos(theta), np.sin(theta)
    legendre = {}
    diagonal = np.full_like(cosine, math.sqrt(1.0 / (4.0 * math.pi)))
    for m in range(ORDER + 1):
        if m > 0:
            diagonal = -math.sqrt((2.0 * m + 1.0) / (2.0 * m)) * sine * diagonal
        legendre[m, m] = diagonal
        if m < ORDER:
            legendre[m + 1, m] = math.sqrt(2.0 * m + 3.0) * cosine * diagonal
        for l in range(m + 2, ORDER + 1):
            one = math.sqrt((4.0 * l * l - 1.0) / (l * l - m * m))
            two = math.sqrt(((l - 1.0) ** 2 - m * m) / (4.0 * (l - 1.0) ** 2 - 1.0))
            legendre[l, m] = one * (cosine * legendre[l - 1, m] - two * legendre[l - 2, m])
    lat = np.zeros((3 * LANES, LANES))
    lon = np.zeros((3 * LANES, LANES))
    row = 0
    for l in range(ORDER + 1):
        for m in range(-l, l + 1):
            lat[row, :LATS] = legendre[l, abs(m)]
            if m == 0:
                wave = np.ones(LONS)
            elif m > 0:
                wave = math.sqrt(2.0) * np.cos(m * phi)
            else:
                wave = math.sqrt(2.0) * np.sin(-m * phi)
            lon[row, :LONS] = wave
            lon[row, LONS:] = wave
            row += 1
    weights = np.zeros((8, PADDED))
    weights[:, :POINTS] = np.repeat(sine * (math.pi / LATS) * (2.0 * math.pi / LONS), LONS) * FACTOR
    return lat.astype(np.float32), lon.astype(np.float32), weights.astype(np.float32)


def pick_kernel(asked_ref, tiles_ref, out_ref):
    def pick(slot, carry):
        source = jnp.maximum(asked_ref[slot], 0)
        out_ref[slot] = tiles_ref[source]
        return carry

    lax.fori_loop(0, out_ref.shape[0], pick, 0, unroll=8)


def pair_kernel(
    slots,
    rows,
    meta_ref,
    offset_ref,
    lat_ref,
    lon_ref,
    weight_ref,
    received_ref,
    low_ref,
    high_ref,
    slot_out,
    low_out,
    high_out,
    source,
    ends,
    basis,
    surface,
    force,
    near_turned,
    near_rows,
    near_side,
    far_rows,
    far_side,
    far_wide,
    far_sum,
    near_wide,
    near_sum,
):
    pairs = meta_ref.shape[0] // 2
    sub = rows // 8
    blocks = POINTS // rows
    count = slots.total
    live = meta_ref[2 * pairs]
    rims = low_ref.shape[0] // 8

    source[: count * 8] = received_ref[...]
    source[count * 8 : (count + rims) * 8] = low_ref[...]
    source[(count + rims) * 8 :] = high_ref[...]
    for pair in range(pairs):
        for side in range(2):
            start = pl.multiple_of(meta_ref[side * pairs + pair] * 8, 8)
            ends[(side * pairs + pair) * 8 : (side * pairs + pair + 1) * 8] = source[pl.ds(start, 8)]

    def chunk(index):
        return ends[pl.ds(index, 2 * pairs, stride=8), :]

    tails = chunk(6)
    tail_rows = [tails, pltpu.roll(tails, LANES // 2, 1), chunk(7)]
    coefs = jnp.concatenate(
        [
            jnp.concatenate([chunk(2 * c), chunk(2 * c + 1), tail_rows[c]], axis=1)
            for c in range(3)
        ],
        axis=0,
    )
    shift = offset_ref[...] * (0.5 * SCALE)
    half = lax.broadcasted_iota(jnp.int32, lat_ref.shape, 1) < LONS
    widest = jnp.zeros((6 * pairs, LANES), F32)
    for t in range(TILES):
        lanes = slice(t * LANES, (t + 1) * LANES)
        lat = jnp.where(half, lat_ref[:, 2 * t : 2 * t + 1], lat_ref[:, 2 * t + 1 : 2 * t + 2])
        table = lat * lon_ref[...]
        basis[:, lanes] = table
        part = jnp.dot(coefs, table, precision=HIGHEST, preferred_element_type=F32)
        part = part * SCALE + shift
        if t == TILES - 1:
            valid = lax.broadcasted_iota(jnp.int32, part.shape, 1) < POINTS - t * LANES
            part = jnp.where(valid, part, 0.0)
        surface[:, lanes] = part
        widest = jnp.maximum(widest, jnp.abs(part))
    reach = jnp.max(widest, axis=1, keepdims=True)
    reach = functools.reduce(
        jnp.maximum, [reach[k * pairs : (k + 1) * pairs] for k in range(6)]
    )
    step = jnp.full_like(reach, 0.25)
    for power in range(-2, 12):
        step = jnp.where(reach > 256.0 * 2.0**power, 2.0 ** (power + 1), step)
    inverse = jnp.full_like(reach, 4.0)
    for power in range(-2, 12):
        inverse = jnp.where(reach > 256.0 * 2.0**power, 2.0 ** -(power + 1), inverse)
    square = step * step

    def rounded(value):
        return value.astype(BF16).astype(F32)

    def in_pieces(value):
        first = rounded(value)
        second = rounded(value - first)
        return [first, second, rounded(value - first - second)]

    def on_grid(values):
        whole = [jnp.round(v * inverse) for v in values]
        rest = [v * inverse - w for v, w in zip(values, whole)]
        upper = [rounded(r) for r in rest]
        lower = [rounded(r - u) for r, u in zip(rest, upper)]
        exact = whole[0] * whole[0] + whole[1] * whole[1] + whole[2] * whole[2]
        small = [2.0 * w * r + r * r for w, r in zip(whole, rest)]
        return whole, upper, lower, exact, small[0] + small[1] + small[2]

    for t in range(TILES):
        lanes = slice(t * LANES, (t + 1) * LANES)
        near = [surface[c * 2 * pairs : c * 2 * pairs + pairs, lanes] for c in range(3)]
        far = [surface[c * 2 * pairs + pairs : (c + 1) * 2 * pairs, lanes] for c in range(3)]
        one = jnp.ones((pairs, LANES), F32)
        scale = jnp.broadcast_to(square, one.shape)

        whole, upper, lower, exact, small = on_grid(near)
        exact, small = in_pieces(exact), in_pieces(small)
        listed = dict(enumerate(exact + [one] * 3 + [-2.0 * v for v in whole]))
        listed.update(enumerate(small + [one] * 3, SMALL))
        for c in range(3):
            n, m, l = -2.0 * whole[c], -2.0 * upper[c], -2.0 * lower[c]
            listed.update(enumerate([n, n, m, l, m, m, l], SMALL + 6 + 7 * c))
        listed.update(enumerate(near, COORDS))
        for k, v in listed.items():
            near_rows[t, pl.ds(k, pairs, stride=FEATURES), :] = v

        whole, upper, lower, exact, small = on_grid(far)
        small = small * square + 1.0
        if t == TILES - 1:
            valid = lax.broadcasted_iota(jnp.int32, small.shape, 1) < POINTS - t * LANES
            small = jnp.where(valid, small, FAR_AWAY)
        whole, upper, lower = [[v * square for v in part] for part in (whole, upper, lower)]
        listed = dict(enumerate([scale] * 3 + in_pieces(exact * square) + whole))
        listed.update(enumerate([scale] * 3 + in_pieces(small), SMALL))
        for c in range(3):
            n, m, l = whole[c], upper[c], lower[c]
            listed.update(enumerate([m, l, n, n, m, l, m], SMALL + 6 + 7 * c))
        for k, v in listed.items():
            far_rows[t, pl.ds(k, pairs, stride=FEATURES), :] = v

    def used(shape, axis, coords):
        feature = lax.rem(lax.broadcasted_iota(jnp.int32, shape, axis), FEATURES)
        keep = (feature < 9) | ((feature >= SMALL) & (feature < SMALL + 27))
        if coords:
            keep = keep | ((feature >= COORDS) & (feature < COORDS + 3))
        return keep

    near_used = used((LANES, LANES), 1, True)

    def turn(t, carry):
        start = pl.multiple_of(t * LANES, LANES)
        for q in range(pairs // 2):
            block = near_rows[t, q * LANES : (q + 1) * LANES, :].T
            near_side[q, pl.ds(start, LANES), :] = jnp.where(near_used, block, 0.0)
        return carry

    lax.fori_loop(0, TILES, turn, 0)
    near_turned[...] = jnp.zeros_like(near_turned)
    force[...] = jnp.zeros_like(force)

    lane_wide = lax.broadcasted_iota(jnp.int32, (rows, LANES), 1)
    far_used = used((FEATURES, LANES), 0, False)

    def one_pair(pair, carry):
        group = pair // 2
        odd = lax.rem(pair, 2)

        def spread(block):
            start = pl.multiple_of(block * rows, 8)
            columns = pltpu.roll(
                near_side[group, pl.ds(start, rows), :], lax.rem(LANES - odd * FEATURES, LANES), 1
            )
            for c in range(3):
                column = columns[:, COORDS + c : COORDS + c + 1]
                near_wide[c] = jnp.broadcast_to(column, (rows, LANES)).reshape(sub, 8, LANES)

        def gather_near(block):
            start = pl.multiple_of(block * rows, 8)
            value = near_turned[pl.ds(start, rows), :]
            for c in range(3):
                total = jnp.sum(near_sum[c].reshape(rows, LANES), axis=1, keepdims=True)
                value = jnp.where(lane_wide == c * pairs + pair, total, value)
            near_turned[pl.ds(start, rows), :] = value

        for c in range(3):
            row = surface[pl.ds(c * 2 * pairs + pairs + pair, 1), :]
            far_wide[c] = jnp.broadcast_to(row, (8, PADDED))
        for t in range(TILES):
            start = pl.multiple_of(pair * FEATURES, FEATURES)
            own = far_rows[t, pl.ds(start, FEATURES), :]
            for side in range(2):
                half_own = jnp.where(far_used & (odd == side), own, 0.0)
                far_side[side * FEATURES : (side + 1) * FEATURES, t * LANES : (t + 1) * LANES] = (
                    half_own.astype(BF16)
                )
        far_sum[...] = jnp.zeros_like(far_sum)
        near_sum[...] = jnp.zeros_like(near_sum)
        spread(0)

        def one_block(block, inner):
            start = pl.multiple_of(block * rows, 8)
            left = near_side[group, pl.ds(start, rows), :].astype(BF16)
            near = [near_wide[c] for c in range(3)]
            gather_near(jnp.maximum(block - 1, 0))
            spread(jnp.minimum(block + 1, blocks - 1))
            near_acc = [jnp.zeros((sub, 8, LANES), F32) for _ in range(3)]
            for first in range(0, TILES, 2):
                last = min(first + 2, TILES)
                grown = jnp.dot(
                    left,
                    far_side[:, first * LANES : last * LANES],
                    preferred_element_type=F32,
                )
                for t in range(first, last):
                    lanes = slice(t * LANES, (t + 1) * LANES)
                    here = slice((t - first) * LANES, (t - first + 1) * LANES)
                    kernel = 1.0 / grown[:, here].reshape(sub, 8, LANES)
                    kernel = kernel * kernel
                    for c in range(3):
                        pull = kernel * (near[c] - far_wide[c, :, lanes][None])
                        near_acc[c] = near_acc[c] + pull
                        far_sum[c, :, lanes] = far_sum[c, :, lanes] + jnp.sum(pull, axis=0)
            for c in range(3):
                near_sum[c] = near_acc[c]
            return inner

        lax.fori_loop(0, blocks, one_block, 0)
        gather_near(blocks - 1)
        for c in range(3):
            force[pl.ds(c * 2 * pairs + pairs + pair, 1), :] = -jnp.sum(
                far_sum[c], axis=0, keepdims=True
            )
        return carry

    lax.fori_loop(0, live, one_pair, 0)

    total = jnp.zeros((6 * pairs, 3 * LANES), F32)
    for t in range(TILES):
        lanes = slice(t * LANES, (t + 1) * LANES)
        near = near_turned[lanes, :].T
        for c in range(3):
            force[c * 2 * pairs : c * 2 * pairs + pairs, lanes] = near[c * pairs : (c + 1) * pairs]
        part = force[:, lanes] * weight_ref[0:1, lanes]
        total = total + lax.dot_general(
            part,
            basis[:, lanes],
            (((1,), (1,)), ((), ())),
            precision=HIGHEST,
            preferred_element_type=F32,
        )
    for c in range(3):
        block = total[c * 2 * pairs : (c + 1) * 2 * pairs]
        ends[pl.ds(2 * c, 2 * pairs, stride=8), :] = block[:, :LANES]
        ends[pl.ds(2 * c + 1, 2 * pairs, stride=8), :] = block[:, LANES : 2 * LANES]
    tail = [total[c * 2 * pairs : (c + 1) * 2 * pairs, 2 * LANES :] for c in range(3)]
    ends[pl.ds(6, 2 * pairs, stride=8), :] = tail[0] + pltpu.roll(tail[1], LANES // 2, 1)
    ends[pl.ds(7, 2 * pairs, stride=8), :] = tail[2]

    source[...] = jnp.zeros_like(source)

    def hand_out(pair, carry):
        for side in range(2):
            value = ends[pl.ds(pl.multiple_of((side * pairs + pair) * 8, 8), 8), :]
            start = pl.multiple_of(meta_ref[side * pairs + pair] * 8, 8)
            source[pl.ds(start, 8), :] = source[pl.ds(start, 8), :] + value
        return carry

    lax.fori_loop(0, live, hand_out, 0)
    slot_out[...] = source[: count * 8]
    low_out[...] = source[count * 8 : (count + rims) * 8]
    high_out[...] = source[(count + rims) * 8 :]


def collect_kernel(asked_ref, returned_ref, low_ref, high_ref, out_ref, total):
    vesicles = out_ref.shape[0]
    total[...] = jnp.zeros_like(total)
    rims = low_ref.shape[0]
    total[:rims] = low_ref[...] + high_ref[...]

    def add(slot, carry):
        asked = asked_ref[slot]
        row = jnp.where(asked >= 0, asked, vesicles)
        total[row] = total[row] + returned_ref[slot]
        return carry

    lax.fori_loop(0, returned_ref.shape[0], add, 0, unroll=4)
    rest = NCOEF - 2 * LANES
    for v in range(vesicles):
        for c in range(3):
            out_ref[v, c : c + 1, :LANES] = total[v, 2 * c : 2 * c + 1, :]
            out_ref[v, c : c + 1, LANES : 2 * LANES] = total[v, 2 * c + 1 : 2 * c + 2, :]
        out_ref[v, 0:1, 2 * LANES :] = total[v, 6:7, :rest]
        moved = pltpu.roll(total[v], LANES // 2, 1)
        out_ref[v, 1:2, 2 * LANES :] = moved[6:7, :rest]
        out_ref[v, 2:3, 2 * LANES :] = total[v, 7:8, :rest]


class Slots:
    def __init__(self, members, cap):
        self.members = members
        self.cap = cap
        self.total = members * cap

    def __repr__(self):
        return "slots"


def vmem():
    return pl.BlockSpec(memory_space=pltpu.VMEM)


def smem():
    return pl.BlockSpec(memory_space=pltpu.SMEM)


def per_device(coefficients, pair_list, pair_offset):
    members = lax.axis_size("member")
    groups = lax.axis_size("group")
    group_here = lax.axis_index("group")
    vesicles = coefficients.shape[0]
    pairs = pair_list.shape[0]
    slots = Slots(members, max(2, (2 * pairs + members - 1) // members))
    total_slots = slots.total
    forward = [(i, i + 1) for i in range(groups - 1)]
    backward = [(i + 1, i) for i in range(groups - 1)]

    end_ids = pair_list.T.reshape(-1)
    end_live = end_ids >= 0
    safe_ids = jnp.maximum(end_ids, 0)
    owner_device = safe_ids // vesicles
    owner_group = owner_device // members
    owner_member = owner_device % members
    owner_slot = safe_ids % vesicles
    inside = end_live & (owner_group == group_here)
    key = jnp.where(inside, owner_member, -1)
    order = jnp.arange(2 * pairs)
    same = (key[:, None] == key[None, :]) & (order[None, :] < order[:, None])
    earlier = jnp.sum(same.astype(jnp.int32), axis=1)
    end_slot = jnp.where(inside, owner_member * slots.cap + earlier, -1)
    hit = end_slot[None, :] == jnp.arange(total_slots)[:, None]
    request = jnp.max(jnp.where(hit, owner_slot[None, :], -1), axis=1)
    asked_for = lax.all_to_all(
        request.reshape(members, slots.cap), "member", split_axis=0, concat_axis=0, tiled=True
    ).reshape(-1)

    head = coefficients[:, :, : 2 * LANES].reshape(vesicles, 6, LANES)
    tail = jnp.pad(coefficients[:, :, 2 * LANES :], ((0, 0), (0, 1), (0, LANES // 2 - (NCOEF - 2 * LANES))))
    tiles = jnp.concatenate([head, tail.reshape(vesicles, 2, LANES)], axis=1)
    rim = tiles[:RIM_VES]
    low = lax.ppermute(rim, "group", forward)
    high = lax.ppermute(rim, "group", backward)

    outgoing = pl.pallas_call(
        pick_kernel,
        out_shape=jax.ShapeDtypeStruct((total_slots, 8, LANES), F32),
        in_specs=[smem(), vmem()],
        out_specs=vmem(),
        name="pick",
    )(asked_for, tiles)
    received = lax.all_to_all(
        outgoing.reshape(members, slots.cap, 8, LANES),
        "member",
        split_axis=0,
        concat_axis=0,
        tiled=True,
    )

    rim_row = (
        total_slots
        + jnp.where(owner_group < group_here, 0, RIM_VES)
        + jnp.minimum(owner_slot, RIM_VES - 1)
    )
    end_row = jnp.where(inside, end_slot, jnp.where(end_live, rim_row, 0))
    live_pairs = jnp.sum((pair_list[:, 0] >= 0).astype(jnp.int32))
    meta = jnp.concatenate([end_row, live_pairs[None]]).astype(jnp.int32)
    offsets = jnp.concatenate([pair_offset.T, -pair_offset.T], axis=1).reshape(-1, 1)

    lat, lon, weights = factor_tables()
    rows = 192
    slot_force, low_force, high_force = pl.pallas_call(
        functools.partial(pair_kernel, slots, rows),
        out_shape=(
            jax.ShapeDtypeStruct((total_slots * 8, LANES), F32),
            jax.ShapeDtypeStruct((RIM_VES * 8, LANES), F32),
            jax.ShapeDtypeStruct((RIM_VES * 8, LANES), F32),
        ),
        in_specs=[smem()] + [vmem()] * 7,
        out_specs=(vmem(),) * 3,
        scratch_shapes=[
            pltpu.VMEM(((total_slots + 2 * RIM_VES) * 8, LANES), F32),
            pltpu.VMEM((2 * pairs * 8, LANES), F32),
            pltpu.VMEM((3 * LANES, PADDED), F32),
            pltpu.VMEM((6 * pairs, PADDED), F32),
            pltpu.VMEM((6 * pairs, PADDED), F32),
            pltpu.VMEM((PADDED, LANES), F32),
            pltpu.VMEM((TILES, pairs * FEATURES, LANES), F32),
            pltpu.VMEM((pairs // 2, PADDED, LANES), F32),
            pltpu.VMEM((TILES, pairs * FEATURES, LANES), F32),
            pltpu.VMEM((2 * FEATURES, PADDED), BF16),
            pltpu.VMEM((3, 8, PADDED), F32),
            pltpu.VMEM((3, 8, PADDED), F32),
            pltpu.VMEM((3, rows // 8, 8, LANES), F32),
            pltpu.VMEM((3, rows // 8, 8, LANES), F32),
        ],
        compiler_params=pltpu.CompilerParams(vmem_limit_bytes=56 << 20),
        name="pair_forces",
    )(
        meta,
        offsets,
        jnp.asarray(lat),
        jnp.asarray(lon),
        jnp.asarray(weights),
        received.reshape(total_slots * 8, LANES),
        low.reshape(RIM_VES * 8, LANES),
        high.reshape(RIM_VES * 8, LANES),
    )
    returned = lax.all_to_all(
        slot_force.reshape(members, slots.cap, 8, LANES),
        "member",
        split_axis=0,
        concat_axis=0,
        tiled=True,
    )
    from_low = lax.ppermute(high_force.reshape(RIM_VES, 8, LANES), "group", forward)
    from_high = lax.ppermute(low_force.reshape(RIM_VES, 8, LANES), "group", backward)
    return pl.pallas_call(
        collect_kernel,
        out_shape=jax.ShapeDtypeStruct(coefficients.shape, F32),
        in_specs=[smem()] + [vmem()] * 3,
        out_specs=vmem(),
        scratch_shapes=[pltpu.VMEM((vesicles + 1, 8, LANES), F32)],
        name="collect",
    )(asked_for, returned.reshape(total_slots, 8, LANES), from_low, from_high)


def solution(mesh):
    return jax.shard_map(
        per_device,
        mesh=mesh,
        in_specs=(
            P(("group", "member"), None, None),
            P(("group", "member"), None),
            P(("group", "member"), None),
        ),
        out_specs=P(("group", "member"), None, None),
        check_vma=False,
    )
```

```python
import functools
import math

import jax
import jax.numpy as jnp
import numpy as np
from jax import lax
from jax.experimental import pallas as pl
from jax.experimental.pallas import tpu as pltpu
from jax.sharding import PartitionSpec as P

ORDER = 16
UPORDER = 32
RIM_VES = 4
LATS = UPORDER + 1
LONS = 2 * UPORDER
POINTS = LATS * LONS
NCOEF = (ORDER + 1) ** 2
LANES = 128
TILES = -(-POINTS // LANES)
PADDED = TILES * LANES
WIDTH = (0.7 * math.pi / LATS) ** 2
SCALE = 1.0 / math.sqrt(WIDTH)
FACTOR = math.sqrt(WIDTH) / (POINTS * WIDTH * WIDTH)
FAR_AWAY = 1e18
F32 = jnp.float32
BF16 = jnp.bfloat16
FEATURES = 64
SMALL = 16
COORDS = 48
HIGHEST = lax.Precision.HIGHEST


def factor_tables():
    theta = (np.arange(LATS) + 0.5) * (math.pi / LATS)
    phi = np.arange(LONS) * (2.0 * math.pi / LONS)
    cosine, sine = np.cos(theta), np.sin(theta)
    legendre = {}
    diagonal = np.full_like(cosine, math.sqrt(1.0 / (4.0 * math.pi)))
    for m in range(ORDER + 1):
        if m > 0:
            diagonal = -math.sqrt((2.0 * m + 1.0) / (2.0 * m)) * sine * diagonal
        legendre[m, m] = diagonal
        if m < ORDER:
            legendre[m + 1, m] = math.sqrt(2.0 * m + 3.0) * cosine * diagonal
        for l in range(m + 2, ORDER + 1):
            one = math.sqrt((4.0 * l * l - 1.0) / (l * l - m * m))
            two = math.sqrt(((l - 1.0) ** 2 - m * m) / (4.0 * (l - 1.0) ** 2 - 1.0))
            legendre[l, m] = one * (cosine * legendre[l - 1, m] - two * legendre[l - 2, m])
    lat = np.zeros((3 * LANES, LANES))
    lon = np.zeros((3 * LANES, LANES))
    row = 0
    for l in range(ORDER + 1):
        for m in range(-l, l + 1):
            lat[row, :LATS] = legendre[l, abs(m)]
            if m == 0:
                wave = np.ones(LONS)
            elif m > 0:
                wave = math.sqrt(2.0) * np.cos(m * phi)
            else:
                wave = math.sqrt(2.0) * np.sin(-m * phi)
            lon[row, :LONS] = wave
            lon[row, LONS:] = wave
            row += 1
    weights = np.zeros((8, PADDED))
    weights[:, :POINTS] = np.repeat(sine * (math.pi / LATS) * (2.0 * math.pi / LONS), LONS) * FACTOR
    return lat.astype(np.float32), lon.astype(np.float32), weights.astype(np.float32)


def pick_kernel(asked_ref, tiles_ref, out_ref):
    def pick(slot, carry):
        source = jnp.maximum(asked_ref[slot], 0)
        out_ref[slot] = tiles_ref[source]
        return carry

    lax.fori_loop(0, out_ref.shape[0], pick, 0, unroll=8)


def pair_kernel(
    slots,
    rows,
    meta_ref,
    offset_ref,
    lat_ref,
    lon_ref,
    weight_ref,
    received_ref,
    low_ref,
    high_ref,
    slot_out,
    low_out,
    high_out,
    source,
    ends,
    basis,
    surface,
    force,
    near_turned,
    near_rows,
    near_side,
    far_rows,
    far_side,
    far_wide,
    far_sum,
    near_wide,
    near_sum,
):
    pairs = meta_ref.shape[0] // 2
    sub = rows // 8
    blocks = POINTS // rows
    count = slots.total
    live = meta_ref[2 * pairs]
    rims = low_ref.shape[0] // 8

    source[: count * 8] = received_ref[...]
    source[count * 8 : (count + rims) * 8] = low_ref[...]
    source[(count + rims) * 8 :] = high_ref[...]
    for pair in range(pairs):
        for side in range(2):
            start = pl.multiple_of(meta_ref[side * pairs + pair] * 8, 8)
            ends[(side * pairs + pair) * 8 : (side * pairs + pair + 1) * 8] = source[pl.ds(start, 8)]

    def chunk(index):
        return ends[pl.ds(index, 2 * pairs, stride=8), :]

    tails = chunk(6)
    tail_rows = [tails, pltpu.roll(tails, LANES // 2, 1), chunk(7)]
    coefs = jnp.concatenate(
        [
            jnp.concatenate([chunk(2 * c), chunk(2 * c + 1), tail_rows[c]], axis=1)
            for c in range(3)
        ],
        axis=0,
    )
    shift = offset_ref[...] * (0.5 * SCALE)
    half = lax.broadcasted_iota(jnp.int32, lat_ref.shape, 1) < LONS
    widest = jnp.zeros((6 * pairs, LANES), F32)
    for t in range(TILES):
        lanes = slice(t * LANES, (t + 1) * LANES)
        lat = jnp.where(half, lat_ref[:, 2 * t : 2 * t + 1], lat_ref[:, 2 * t + 1 : 2 * t + 2])
        table = lat * lon_ref[...]
        basis[:, lanes] = table
        part = jnp.dot(coefs, table, precision=HIGHEST, preferred_element_type=F32)
        part = part * SCALE + shift
        if t == TILES - 1:
            valid = lax.broadcasted_iota(jnp.int32, part.shape, 1) < POINTS - t * LANES
            part = jnp.where(valid, part, 0.0)
        surface[:, lanes] = part
        widest = jnp.maximum(widest, jnp.abs(part))
    reach = jnp.max(widest, axis=1, keepdims=True)
    reach = functools.reduce(
        jnp.maximum, [reach[k * pairs : (k + 1) * pairs] for k in range(6)]
    )
    step = jnp.full_like(reach, 0.25)
    for power in range(-2, 12):
        step = jnp.where(reach > 256.0 * 2.0**power, 2.0 ** (power + 1), step)
    inverse = jnp.full_like(reach, 4.0)
    for power in range(-2, 12):
        inverse = jnp.where(reach > 256.0 * 2.0**power, 2.0 ** -(power + 1), inverse)
    square = step * step

    def rounded(value):
        return value.astype(BF16).astype(F32)

    def in_pieces(value):
        first = rounded(value)
        second = rounded(value - first)
        return [first, second, rounded(value - first - second)]

    def on_grid(values):
        whole = [jnp.round(v * inverse) for v in values]
        rest = [v * inverse - w for v, w in zip(values, whole)]
        upper = [rounded(r) for r in rest]
        lower = [rounded(r - u) for r, u in zip(rest, upper)]
        exact = whole[0] * whole[0] + whole[1] * whole[1] + whole[2] * whole[2]
        small = [2.0 * w * r + r * r for w, r in zip(whole, rest)]
        return whole, upper, lower, exact, small[0] + small[1] + small[2]

    def used(shape, axis, coords):
        feature = lax.rem(lax.broadcasted_iota(jnp.int32, shape, axis), FEATURES)
        keep = (feature < 9) | ((feature >= SMALL) & (feature < SMALL + 27))
        if coords:
            keep = keep | ((feature >= COORDS) & (feature < COORDS + 3))
        return keep

    near_used = used((LANES, LANES), 1, True)

    for t in range(TILES):
        lanes = slice(t * LANES, (t + 1) * LANES)
        near = [surface[c * 2 * pairs : c * 2 * pairs + pairs, lanes] for c in range(3)]
        far = [surface[c * 2 * pairs + pairs : (c + 1) * 2 * pairs, lanes] for c in range(3)]
        one = jnp.ones((pairs, LANES), F32)
        scale = jnp.broadcast_to(square, one.shape)

        whole, upper, lower, exact, small = on_grid(near)
        exact, small = in_pieces(exact), in_pieces(small)
        listed = dict(enumerate(exact + [one] * 3 + [-2.0 * v for v in whole]))
        listed.update(enumerate(small + [one] * 3, SMALL))
        for c in range(3):
            n, m, l = -2.0 * whole[c], -2.0 * upper[c], -2.0 * lower[c]
            listed.update(enumerate([n, n, m, l, m, m, l], SMALL + 6 + 7 * c))
        listed.update(enumerate(near, COORDS))
        for k, v in listed.items():
            near_rows[t, pl.ds(k, pairs, stride=FEATURES), :] = v
        for q in range(pairs // 2):
            block = near_rows[t, q * LANES : (q + 1) * LANES, :].T
            near_side[q, lanes, :] = jnp.where(near_used, block, 0.0)

        whole, upper, lower, exact, small = on_grid(far)
        small = small * square + 1.0
        if t == TILES - 1:
            valid = lax.broadcasted_iota(jnp.int32, small.shape, 1) < POINTS - t * LANES
            small = jnp.where(valid, small, FAR_AWAY)
        whole, upper, lower = [[v * square for v in part] for part in (whole, upper, lower)]
        listed = dict(enumerate([scale] * 3 + in_pieces(exact * square) + whole))
        listed.update(enumerate([scale] * 3 + in_pieces(small), SMALL))
        for c in range(3):
            n, m, l = whole[c], upper[c], lower[c]
            listed.update(enumerate([m, l, n, n, m, l, m], SMALL + 6 + 7 * c))
        for k, v in listed.items():
            far_rows[t, pl.ds(k, pairs, stride=FEATURES), :] = v

    near_turned[...] = jnp.zeros_like(near_turned)
    force[...] = jnp.zeros_like(force)

    lane_wide = lax.broadcasted_iota(jnp.int32, (rows, LANES), 1)
    far_used = used((FEATURES, LANES), 0, False)

    def one_pair(pair, carry):
        group = pair // 2
        odd = lax.rem(pair, 2)

        def spread(block):
            start = pl.multiple_of(block * rows, 8)
            columns = pltpu.roll(
                near_side[group, pl.ds(start, rows), :], lax.rem(LANES - odd * FEATURES, LANES), 1
            )
            for c in range(3):
                column = columns[:, COORDS + c : COORDS + c + 1]
                near_wide[c] = jnp.broadcast_to(column, (rows, LANES)).reshape(sub, 8, LANES)

        def gather_near(block):
            start = pl.multiple_of(block * rows, 8)
            value = near_turned[pl.ds(start, rows), :]
            for c in range(3):
                total = jnp.sum(near_sum[c].reshape(rows, LANES), axis=1, keepdims=True)
                value = jnp.where(lane_wide == c * pairs + pair, total, value)
            near_turned[pl.ds(start, rows), :] = value

        for c in range(3):
            row = surface[pl.ds(c * 2 * pairs + pairs + pair, 1), :]
            far_wide[c] = jnp.broadcast_to(row, (8, PADDED))
        for t in range(TILES):
            start = pl.multiple_of(pair * FEATURES, FEATURES)
            own = far_rows[t, pl.ds(start, FEATURES), :]
            for side in range(2):
                half_own = jnp.where(far_used & (odd == side), own, 0.0)
                far_side[side * FEATURES : (side + 1) * FEATURES, t * LANES : (t + 1) * LANES] = (
                    half_own.astype(BF16)
                )
        far_sum[...] = jnp.zeros_like(far_sum)
        near_sum[...] = jnp.zeros_like(near_sum)
        spread(0)

        def one_block(block, inner):
            start = pl.multiple_of(block * rows, 8)
            left = near_side[group, pl.ds(start, rows), :].astype(BF16)
            near = [near_wide[c] for c in range(3)]
            gather_near(jnp.maximum(block - 1, 0))
            spread(jnp.minimum(block + 1, blocks - 1))
            near_acc = [jnp.zeros((sub, 8, LANES), F32) for _ in range(3)]
            for first in range(0, TILES, 2):
                last = min(first + 2, TILES)
                grown = jnp.dot(
                    left,
                    far_side[:, first * LANES : last * LANES],
                    preferred_element_type=F32,
                )
                for t in range(first, last):
                    lanes = slice(t * LANES, (t + 1) * LANES)
                    here = slice((t - first) * LANES, (t - first + 1) * LANES)
                    kernel = 1.0 / grown[:, here].reshape(sub, 8, LANES)
                    kernel = kernel * kernel
                    for c in range(3):
                        pull = kernel * (near[c] - far_wide[c, :, lanes][None])
                        near_acc[c] = near_acc[c] + pull
                        far_sum[c, :, lanes] = far_sum[c, :, lanes] + jnp.sum(pull, axis=0)
            for c in range(3):
                near_sum[c] = near_acc[c]
            return inner

        lax.fori_loop(0, blocks, one_block, 0)
        gather_near(blocks - 1)
        for c in range(3):
            force[pl.ds(c * 2 * pairs + pairs + pair, 1), :] = -jnp.sum(
                far_sum[c], axis=0, keepdims=True
            )
        return carry

    lax.fori_loop(0, live, one_pair, 0)

    total = jnp.zeros((6 * pairs, 3 * LANES), F32)
    for t in range(TILES):
        lanes = slice(t * LANES, (t + 1) * LANES)
        near = near_turned[lanes, :].T
        for c in range(3):
            force[c * 2 * pairs : c * 2 * pairs + pairs, lanes] = near[c * pairs : (c + 1) * pairs]
        part = force[:, lanes] * weight_ref[0:1, lanes]
        total = total + lax.dot_general(
            part,
            basis[:, lanes],
            (((1,), (1,)), ((), ())),
            precision=HIGHEST,
            preferred_element_type=F32,
        )
    for c in range(3):
        block = total[c * 2 * pairs : (c + 1) * 2 * pairs]
        ends[pl.ds(2 * c, 2 * pairs, stride=8), :] = block[:, :LANES]
        ends[pl.ds(2 * c + 1, 2 * pairs, stride=8), :] = block[:, LANES : 2 * LANES]
    tail = [total[c * 2 * pairs : (c + 1) * 2 * pairs, 2 * LANES :] for c in range(3)]
    ends[pl.ds(6, 2 * pairs, stride=8), :] = tail[0] + pltpu.roll(tail[1], LANES // 2, 1)
    ends[pl.ds(7, 2 * pairs, stride=8), :] = tail[2]

    source[...] = jnp.zeros_like(source)

    def hand_out(pair, carry):
        for side in range(2):
            value = ends[pl.ds(pl.multiple_of((side * pairs + pair) * 8, 8), 8), :]
            start = pl.multiple_of(meta_ref[side * pairs + pair] * 8, 8)
            source[pl.ds(start, 8), :] = source[pl.ds(start, 8), :] + value
        return carry

    lax.fori_loop(0, live, hand_out, 0)
    slot_out[...] = source[: count * 8]
    low_out[...] = source[count * 8 : (count + rims) * 8]
    high_out[...] = source[(count + rims) * 8 :]


def collect_kernel(asked_ref, returned_ref, low_ref, high_ref, out_ref, total):
    vesicles = out_ref.shape[0]
    total[...] = jnp.zeros_like(total)
    rims = low_ref.shape[0]
    total[:rims] = low_ref[...] + high_ref[...]

    def add(slot, carry):
        asked = asked_ref[slot]
        row = jnp.where(asked >= 0, asked, vesicles)
        total[row] = total[row] + returned_ref[slot]
        return carry

    lax.fori_loop(0, returned_ref.shape[0], add, 0, unroll=4)
    rest = NCOEF - 2 * LANES
    for v in range(vesicles):
        for c in range(3):
            out_ref[v, c : c + 1, :LANES] = total[v, 2 * c : 2 * c + 1, :]
            out_ref[v, c : c + 1, LANES : 2 * LANES] = total[v, 2 * c + 1 : 2 * c + 2, :]
        out_ref[v, 0:1, 2 * LANES :] = total[v, 6:7, :rest]
        moved = pltpu.roll(total[v], LANES // 2, 1)
        out_ref[v, 1:2, 2 * LANES :] = moved[6:7, :rest]
        out_ref[v, 2:3, 2 * LANES :] = total[v, 7:8, :rest]


class Slots:
    def __init__(self, members, cap):
        self.members = members
        self.cap = cap
        self.total = members * cap

    def __repr__(self):
        return "slots"


def vmem():
    return pl.BlockSpec(memory_space=pltpu.VMEM)


def smem():
    return pl.BlockSpec(memory_space=pltpu.SMEM)


def per_device(coefficients, pair_list, pair_offset):
    members = lax.axis_size("member")
    groups = lax.axis_size("group")
    group_here = lax.axis_index("group")
    vesicles = coefficients.shape[0]
    pairs = pair_list.shape[0]
    slots = Slots(members, max(2, (2 * pairs + members - 1) // members))
    total_slots = slots.total
    forward = [(i, i + 1) for i in range(groups - 1)]
    backward = [(i + 1, i) for i in range(groups - 1)]

    end_ids = pair_list.T.reshape(-1)
    end_live = end_ids >= 0
    safe_ids = jnp.maximum(end_ids, 0)
    owner_device = safe_ids // vesicles
    owner_group = owner_device // members
    owner_member = owner_device % members
    owner_slot = safe_ids % vesicles
    inside = end_live & (owner_group == group_here)
    key = jnp.where(inside, owner_member, -1)
    order = jnp.arange(2 * pairs)
    same = (key[:, None] == key[None, :]) & (order[None, :] < order[:, None])
    earlier = jnp.sum(same.astype(jnp.int32), axis=1)
    end_slot = jnp.where(inside, owner_member * slots.cap + earlier, -1)
    hit = end_slot[None, :] == jnp.arange(total_slots)[:, None]
    request = jnp.max(jnp.where(hit, owner_slot[None, :], -1), axis=1)
    asked_for = lax.all_to_all(
        request.reshape(members, slots.cap), "member", split_axis=0, concat_axis=0, tiled=True
    ).reshape(-1)

    head = coefficients[:, :, : 2 * LANES].reshape(vesicles, 6, LANES)
    tail = jnp.pad(coefficients[:, :, 2 * LANES :], ((0, 0), (0, 1), (0, LANES // 2 - (NCOEF - 2 * LANES))))
    tiles = jnp.concatenate([head, tail.reshape(vesicles, 2, LANES)], axis=1)
    rim = tiles[:RIM_VES]
    low = lax.ppermute(rim, "group", forward)
    high = lax.ppermute(rim, "group", backward)

    outgoing = pl.pallas_call(
        pick_kernel,
        out_shape=jax.ShapeDtypeStruct((total_slots, 8, LANES), F32),
        in_specs=[smem(), vmem()],
        out_specs=vmem(),
        name="pick",
    )(asked_for, tiles)
    received = lax.all_to_all(
        outgoing.reshape(members, slots.cap, 8, LANES),
        "member",
        split_axis=0,
        concat_axis=0,
        tiled=True,
    )

    rim_row = (
        total_slots
        + jnp.where(owner_group < group_here, 0, RIM_VES)
        + jnp.minimum(owner_slot, RIM_VES - 1)
    )
    end_row = jnp.where(inside, end_slot, jnp.where(end_live, rim_row, 0))
    live_pairs = jnp.sum((pair_list[:, 0] >= 0).astype(jnp.int32))
    meta = jnp.concatenate([end_row, live_pairs[None]]).astype(jnp.int32)
    offsets = jnp.concatenate([pair_offset.T, -pair_offset.T], axis=1).reshape(-1, 1)

    lat, lon, weights = factor_tables()
    rows = 264
    slot_force, low_force, high_force = pl.pallas_call(
        functools.partial(pair_kernel, slots, rows),
        out_shape=(
            jax.ShapeDtypeStruct((total_slots * 8, LANES), F32),
            jax.ShapeDtypeStruct((RIM_VES * 8, LANES), F32),
            jax.ShapeDtypeStruct((RIM_VES * 8, LANES), F32),
        ),
        in_specs=[smem()] + [vmem()] * 7,
        out_specs=(vmem(),) * 3,
        scratch_shapes=[
            pltpu.VMEM(((total_slots + 2 * RIM_VES) * 8, LANES), F32),
            pltpu.VMEM((2 * pairs * 8, LANES), F32),
            pltpu.VMEM((3 * LANES, PADDED), F32),
            pltpu.VMEM((6 * pairs, PADDED), F32),
            pltpu.VMEM((6 * pairs, PADDED), F32),
            pltpu.VMEM((PADDED, LANES), F32),
            pltpu.VMEM((TILES, pairs * FEATURES, LANES), F32),
            pltpu.VMEM((pairs // 2, PADDED, LANES), F32),
            pltpu.VMEM((TILES, pairs * FEATURES, LANES), F32),
            pltpu.VMEM((2 * FEATURES, PADDED), BF16),
            pltpu.VMEM((3, 8, PADDED), F32),
            pltpu.VMEM((3, 8, PADDED), F32),
            pltpu.VMEM((3, rows // 8, 8, LANES), F32),
            pltpu.VMEM((3, rows // 8, 8, LANES), F32),
        ],
        compiler_params=pltpu.CompilerParams(vmem_limit_bytes=56 << 20),
        name="pair_forces",
    )(
        meta,
        offsets,
        jnp.asarray(lat),
        jnp.asarray(lon),
        jnp.asarray(weights),
        received.reshape(total_slots * 8, LANES),
        low.reshape(RIM_VES * 8, LANES),
        high.reshape(RIM_VES * 8, LANES),
    )
    returned = lax.all_to_all(
        slot_force.reshape(members, slots.cap, 8, LANES),
        "member",
        split_axis=0,
        concat_axis=0,
        tiled=True,
    )
    from_low = lax.ppermute(high_force.reshape(RIM_VES, 8, LANES), "group", forward)
    from_high = lax.ppermute(low_force.reshape(RIM_VES, 8, LANES), "group", backward)
    return pl.pallas_call(
        collect_kernel,
        out_shape=jax.ShapeDtypeStruct(coefficients.shape, F32),
        in_specs=[smem()] + [vmem()] * 3,
        out_specs=vmem(),
        scratch_shapes=[pltpu.VMEM((vesicles + 1, 8, LANES), F32)],
        name="collect",
    )(asked_for, returned.reshape(total_slots, 8, LANES), from_low, from_high)


def solution(mesh):
    return jax.shard_map(
        per_device,
        mesh=mesh,
        in_specs=(
            P(("group", "member"), None, None),
            P(("group", "member"), None),
            P(("group", "member"), None),
        ),
        out_specs=P(("group", "member"), None, None),
        check_vma=False,
    )
```

```python
import functools
import math

import jax
import jax.numpy as jnp
import numpy as np
from jax import lax
from jax.experimental import pallas as pl
from jax.experimental.pallas import tpu as pltpu
from jax.sharding import PartitionSpec as P

ORDER = 16
UPORDER = 32
RIM_VES = 4
LATS = UPORDER + 1
LONS = 2 * UPORDER
POINTS = LATS * LONS
NCOEF = (ORDER + 1) ** 2
LANES = 128
TILES = -(-POINTS // LANES)
PADDED = TILES * LANES
WIDTH = (0.7 * math.pi / LATS) ** 2
SCALE = 1.0 / math.sqrt(WIDTH)
FACTOR = math.sqrt(WIDTH) / (POINTS * WIDTH * WIDTH)
FAR_AWAY = 1e18
F32 = jnp.float32
BF16 = jnp.bfloat16
FEATURES = 64
SMALL = 16
COORDS = 48
HIGHEST = lax.Precision.HIGHEST


def factor_tables():
    theta = (np.arange(LATS) + 0.5) * (math.pi / LATS)
    phi = np.arange(LONS) * (2.0 * math.pi / LONS)
    cosine, sine = np.cos(theta), np.sin(theta)
    legendre = {}
    diagonal = np.full_like(cosine, math.sqrt(1.0 / (4.0 * math.pi)))
    for m in range(ORDER + 1):
        if m > 0:
            diagonal = -math.sqrt((2.0 * m + 1.0) / (2.0 * m)) * sine * diagonal
        legendre[m, m] = diagonal
        if m < ORDER:
            legendre[m + 1, m] = math.sqrt(2.0 * m + 3.0) * cosine * diagonal
        for l in range(m + 2, ORDER + 1):
            one = math.sqrt((4.0 * l * l - 1.0) / (l * l - m * m))
            two = math.sqrt(((l - 1.0) ** 2 - m * m) / (4.0 * (l - 1.0) ** 2 - 1.0))
            legendre[l, m] = one * (cosine * legendre[l - 1, m] - two * legendre[l - 2, m])
    lat = np.zeros((3 * LANES, LANES))
    lon = np.zeros((3 * LANES, LANES))
    row = 0
    for l in range(ORDER + 1):
        for m in range(-l, l + 1):
            lat[row, :LATS] = legendre[l, abs(m)]
            if m == 0:
                wave = np.ones(LONS)
            elif m > 0:
                wave = math.sqrt(2.0) * np.cos(m * phi)
            else:
                wave = math.sqrt(2.0) * np.sin(-m * phi)
            lon[row, :LONS] = wave
            lon[row, LONS:] = wave
            row += 1
    weights = np.zeros((8, PADDED))
    weights[:, :POINTS] = np.repeat(sine * (math.pi / LATS) * (2.0 * math.pi / LONS), LONS) * FACTOR
    return lat.astype(np.float32), lon.astype(np.float32), weights.astype(np.float32)


def pick_kernel(asked_ref, tiles_ref, out_ref):
    def pick(slot, carry):
        source = jnp.maximum(asked_ref[slot], 0)
        out_ref[slot] = tiles_ref[source]
        return carry

    lax.fori_loop(0, out_ref.shape[0], pick, 0, unroll=8)


def pair_kernel(
    slots,
    rows,
    meta_ref,
    offset_ref,
    lat_ref,
    lon_ref,
    weight_ref,
    received_ref,
    low_ref,
    high_ref,
    slot_out,
    low_out,
    high_out,
    source,
    ends,
    basis,
    surface,
    force,
    near_turned,
    near_rows,
    near_side,
    far_rows,
    far_side,
    far_wide,
    far_sum,
    near_wide,
    near_sum,
):
    pairs = meta_ref.shape[0] // 2
    sub = rows // 8
    blocks = POINTS // rows
    count = slots.total
    live = meta_ref[2 * pairs]
    rims = low_ref.shape[0] // 8

    source[: count * 8] = received_ref[...]
    source[count * 8 : (count + rims) * 8] = low_ref[...]
    source[(count + rims) * 8 :] = high_ref[...]
    for pair in range(pairs):
        for side in range(2):
            start = pl.multiple_of(meta_ref[side * pairs + pair] * 8, 8)
            ends[(side * pairs + pair) * 8 : (side * pairs + pair + 1) * 8] = source[pl.ds(start, 8)]

    def chunk(index):
        return ends[pl.ds(index, 2 * pairs, stride=8), :]

    tails = chunk(6)
    tail_rows = [tails, pltpu.roll(tails, LANES // 2, 1), chunk(7)]
    coefs = jnp.concatenate(
        [
            jnp.concatenate([chunk(2 * c), chunk(2 * c + 1), tail_rows[c]], axis=1)
            for c in range(3)
        ],
        axis=0,
    )
    shift = offset_ref[...] * (0.5 * SCALE)
    half = lax.broadcasted_iota(jnp.int32, lat_ref.shape, 1) < LONS
    widest = jnp.zeros((6 * pairs, LANES), F32)
    for t in range(TILES):
        lanes = slice(t * LANES, (t + 1) * LANES)
        lat = jnp.where(half, lat_ref[:, 2 * t : 2 * t + 1], lat_ref[:, 2 * t + 1 : 2 * t + 2])
        table = lat * lon_ref[...]
        basis[:, lanes] = table
        part = jnp.dot(coefs, table, precision=HIGHEST, preferred_element_type=F32)
        part = part * SCALE + shift
        if t == TILES - 1:
            valid = lax.broadcasted_iota(jnp.int32, part.shape, 1) < POINTS - t * LANES
            part = jnp.where(valid, part, 0.0)
        surface[:, lanes] = part
        widest = jnp.maximum(widest, jnp.abs(part))
    reach = jnp.max(widest, axis=1, keepdims=True)
    reach = functools.reduce(
        jnp.maximum, [reach[k * pairs : (k + 1) * pairs] for k in range(6)]
    )
    step = jnp.full_like(reach, 0.25)
    for power in range(-2, 12):
        step = jnp.where(reach > 256.0 * 2.0**power, 2.0 ** (power + 1), step)
    inverse = jnp.full_like(reach, 4.0)
    for power in range(-2, 12):
        inverse = jnp.where(reach > 256.0 * 2.0**power, 2.0 ** -(power + 1), inverse)
    square = step * step

    def rounded(value):
        return value.astype(BF16).astype(F32)

    def in_pieces(value):
        first = rounded(value)
        second = rounded(value - first)
        return [first, second, rounded(value - first - second)]

    def on_grid(values):
        whole = [jnp.round(v * inverse) for v in values]
        rest = [v * inverse - w for v, w in zip(values, whole)]
        upper = [rounded(r) for r in rest]
        lower = [rounded(r - u) for r, u in zip(rest, upper)]
        exact = whole[0] * whole[0] + whole[1] * whole[1] + whole[2] * whole[2]
        small = [2.0 * w * r + r * r for w, r in zip(whole, rest)]
        return whole, upper, lower, exact, small[0] + small[1] + small[2]

    def used(shape, axis, coords):
        feature = lax.rem(lax.broadcasted_iota(jnp.int32, shape, axis), FEATURES)
        keep = (feature < 9) | ((feature >= SMALL) & (feature < SMALL + 27))
        if coords:
            keep = keep | ((feature >= COORDS) & (feature < COORDS + 3))
        return keep

    near_used = used((LANES, LANES), 1, True)
    feature = lax.rem(lax.broadcasted_iota(jnp.int32, (LANES, LANES), 1), FEATURES)
    near_one = ((feature >= 3) & (feature < 6)) | ((feature >= SMALL + 3) & (feature < SMALL + 6))

    for t in range(TILES):
        lanes = slice(t * LANES, (t + 1) * LANES)
        near = [surface[c * 2 * pairs : c * 2 * pairs + pairs, lanes] for c in range(3)]
        far = [surface[c * 2 * pairs + pairs : (c + 1) * 2 * pairs, lanes] for c in range(3)]
        one = jnp.ones((pairs, LANES), F32)
        scale = jnp.broadcast_to(square, one.shape)

        whole, upper, lower, exact, small = on_grid(near)
        exact, small = in_pieces(exact), in_pieces(small)
        listed = dict(enumerate(exact))
        listed.update(enumerate([-2.0 * v for v in whole], 6))
        listed.update(enumerate(small, SMALL))
        for c in range(3):
            n, m, l = -2.0 * whole[c], -2.0 * upper[c], -2.0 * lower[c]
            listed.update(enumerate([n, n, m, l, m, m, l], SMALL + 6 + 7 * c))
        listed.update(enumerate(near, COORDS))
        for k, v in listed.items():
            near_rows[t, pl.ds(k, pairs, stride=FEATURES), :] = v
        for q in range(pairs // 2):
            block = near_rows[t, q * LANES : (q + 1) * LANES, :].T
            near_side[q, lanes, :] = jnp.where(near_one, 1.0, jnp.where(near_used, block, 0.0))

        whole, upper, lower, exact, small = on_grid(far)
        small = small * square + 1.0
        if t == TILES - 1:
            valid = lax.broadcasted_iota(jnp.int32, small.shape, 1) < POINTS - t * LANES
            small = jnp.where(valid, small, FAR_AWAY)
        whole, upper, lower = [[v * square for v in part] for part in (whole, upper, lower)]
        listed = dict(enumerate([scale] * 3 + in_pieces(exact * square) + whole))
        listed.update(enumerate([scale] * 3 + in_pieces(small), SMALL))
        for c in range(3):
            n, m, l = whole[c], upper[c], lower[c]
            listed.update(enumerate([m, l, n, n, m, l, m], SMALL + 6 + 7 * c))
        for k, v in listed.items():
            far_rows[t, pl.ds(k, pairs, stride=FEATURES), :] = v

    near_turned[...] = jnp.zeros_like(near_turned)
    force[...] = jnp.zeros_like(force)

    lane_wide = lax.broadcasted_iota(jnp.int32, (rows, LANES), 1)
    far_used = used((FEATURES, LANES), 0, False)

    def one_pair(pair, carry):
        group = pair // 2
        odd = lax.rem(pair, 2)

        def spread(block):
            start = pl.multiple_of(block * rows, 8)
            columns = pltpu.roll(
                near_side[group, pl.ds(start, rows), :], lax.rem(LANES - odd * FEATURES, LANES), 1
            )
            for c in range(3):
                column = columns[:, COORDS + c : COORDS + c + 1]
                near_wide[c] = jnp.broadcast_to(column, (rows, LANES)).reshape(sub, 8, LANES)

        def gather_near(block):
            start = pl.multiple_of(block * rows, 8)
            value = near_turned[pl.ds(start, rows), :]
            for c in range(3):
                total = jnp.sum(near_sum[c].reshape(rows, LANES), axis=1, keepdims=True)
                value = jnp.where(lane_wide == c * pairs + pair, total, value)
            near_turned[pl.ds(start, rows), :] = value

        for c in range(3):
            row = surface[pl.ds(c * 2 * pairs + pairs + pair, 1), :]
            far_wide[c] = jnp.broadcast_to(row, (8, PADDED))
        for t in range(TILES):
            start = pl.multiple_of(pair * FEATURES, FEATURES)
            own = far_rows[t, pl.ds(start, FEATURES), :]
            for side in range(2):
                half_own = jnp.where(far_used & (odd == side), own, 0.0)
                far_side[side * FEATURES : (side + 1) * FEATURES, t * LANES : (t + 1) * LANES] = (
                    half_own.astype(BF16)
                )
        far_sum[...] = jnp.zeros_like(far_sum)
        near_sum[...] = jnp.zeros_like(near_sum)
        spread(0)

        def one_block(block, inner):
            start = pl.multiple_of(block * rows, 8)
            left = near_side[group, pl.ds(start, rows), :].astype(BF16)
            near = [near_wide[c] for c in range(3)]
            gather_near(jnp.maximum(block - 1, 0))
            spread(jnp.minimum(block + 1, blocks - 1))
            near_acc = [jnp.zeros((sub, 8, LANES), F32) for _ in range(3)]
            for first in range(0, TILES, 2):
                last = min(first + 2, TILES)
                grown = jnp.dot(
                    left,
                    far_side[:, first * LANES : last * LANES],
                    preferred_element_type=F32,
                )
                for t in range(first, last):
                    lanes = slice(t * LANES, (t + 1) * LANES)
                    here = slice((t - first) * LANES, (t - first + 1) * LANES)
                    kernel = 1.0 / grown[:, here].reshape(sub, 8, LANES)
                    kernel = kernel * kernel
                    for c in range(3):
                        pull = kernel * (near[c] - far_wide[c, :, lanes][None])
                        near_acc[c] = near_acc[c] + pull
                        far_sum[c, :, lanes] = far_sum[c, :, lanes] + jnp.sum(pull, axis=0)
            for c in range(3):
                near_sum[c] = near_acc[c]
            return inner

        lax.fori_loop(0, blocks, one_block, 0)
        gather_near(blocks - 1)
        for c in range(3):
            force[pl.ds(c * 2 * pairs + pairs + pair, 1), :] = -jnp.sum(
                far_sum[c], axis=0, keepdims=True
            )
        return carry

    lax.fori_loop(0, live, one_pair, 0)

    total = jnp.zeros((6 * pairs, 3 * LANES), F32)
    for t in range(TILES):
        lanes = slice(t * LANES, (t + 1) * LANES)
        near = near_turned[lanes, :].T
        for c in range(3):
            force[c * 2 * pairs : c * 2 * pairs + pairs, lanes] = near[c * pairs : (c + 1) * pairs]
        part = force[:, lanes] * weight_ref[0:1, lanes]
        total = total + lax.dot_general(
            part,
            basis[:, lanes],
            (((1,), (1,)), ((), ())),
            precision=HIGHEST,
            preferred_element_type=F32,
        )
    for c in range(3):
        block = total[c * 2 * pairs : (c + 1) * 2 * pairs]
        ends[pl.ds(2 * c, 2 * pairs, stride=8), :] = block[:, :LANES]
        ends[pl.ds(2 * c + 1, 2 * pairs, stride=8), :] = block[:, LANES : 2 * LANES]
    tail = [total[c * 2 * pairs : (c + 1) * 2 * pairs, 2 * LANES :] for c in range(3)]
    ends[pl.ds(6, 2 * pairs, stride=8), :] = tail[0] + pltpu.roll(tail[1], LANES // 2, 1)
    ends[pl.ds(7, 2 * pairs, stride=8), :] = tail[2]

    source[...] = jnp.zeros_like(source)

    def hand_out(pair, carry):
        for side in range(2):
            value = ends[pl.ds(pl.multiple_of((side * pairs + pair) * 8, 8), 8), :]
            start = pl.multiple_of(meta_ref[side * pairs + pair] * 8, 8)
            source[pl.ds(start, 8), :] = source[pl.ds(start, 8), :] + value
        return carry

    lax.fori_loop(0, live, hand_out, 0)
    slot_out[...] = source[: count * 8]
    low_out[...] = source[count * 8 : (count + rims) * 8]
    high_out[...] = source[(count + rims) * 8 :]


def collect_kernel(asked_ref, returned_ref, low_ref, high_ref, out_ref, total):
    vesicles = out_ref.shape[0]
    total[...] = jnp.zeros_like(total)
    rims = low_ref.shape[0]
    total[:rims] = low_ref[...] + high_ref[...]

    def add(slot, carry):
        asked = asked_ref[slot]
        row = jnp.where(asked >= 0, asked, vesicles)
        total[row] = total[row] + returned_ref[slot]
        return carry

    lax.fori_loop(0, returned_ref.shape[0], add, 0, unroll=4)
    rest = NCOEF - 2 * LANES
    for v in range(vesicles):
        for c in range(3):
            out_ref[v, c : c + 1, :LANES] = total[v, 2 * c : 2 * c + 1, :]
            out_ref[v, c : c + 1, LANES : 2 * LANES] = total[v, 2 * c + 1 : 2 * c + 2, :]
        out_ref[v, 0:1, 2 * LANES :] = total[v, 6:7, :rest]
        moved = pltpu.roll(total[v], LANES // 2, 1)
        out_ref[v, 1:2, 2 * LANES :] = moved[6:7, :rest]
        out_ref[v, 2:3, 2 * LANES :] = total[v, 7:8, :rest]


class Slots:
    def __init__(self, members, cap):
        self.members = members
        self.cap = cap
        self.total = members * cap

    def __repr__(self):
        return "slots"


def vmem():
    return pl.BlockSpec(memory_space=pltpu.VMEM)


def smem():
    return pl.BlockSpec(memory_space=pltpu.SMEM)


def per_device(coefficients, pair_list, pair_offset):
    members = lax.axis_size("member")
    groups = lax.axis_size("group")
    group_here = lax.axis_index("group")
    vesicles = coefficients.shape[0]
    pairs = pair_list.shape[0]
    slots = Slots(members, max(2, (2 * pairs + members - 1) // members))
    total_slots = slots.total
    forward = [(i, i + 1) for i in range(groups - 1)]
    backward = [(i + 1, i) for i in range(groups - 1)]

    end_ids = pair_list.T.reshape(-1)
    end_live = end_ids >= 0
    safe_ids = jnp.maximum(end_ids, 0)
    owner_device = safe_ids // vesicles
    owner_group = owner_device // members
    owner_member = owner_device % members
    owner_slot = safe_ids % vesicles
    inside = end_live & (owner_group == group_here)
    key = jnp.where(inside, owner_member, -1)
    order = jnp.arange(2 * pairs)
    same = (key[:, None] == key[None, :]) & (order[None, :] < order[:, None])
    earlier = jnp.sum(same.astype(jnp.int32), axis=1)
    end_slot = jnp.where(inside, owner_member * slots.cap + earlier, -1)
    hit = end_slot[None, :] == jnp.arange(total_slots)[:, None]
    request = jnp.max(jnp.where(hit, owner_slot[None, :], -1), axis=1)
    asked_for = lax.all_to_all(
        request.reshape(members, slots.cap), "member", split_axis=0, concat_axis=0, tiled=True
    ).reshape(-1)

    head = coefficients[:, :, : 2 * LANES].reshape(vesicles, 6, LANES)
    tail = jnp.pad(coefficients[:, :, 2 * LANES :], ((0, 0), (0, 1), (0, LANES // 2 - (NCOEF - 2 * LANES))))
    tiles = jnp.concatenate([head, tail.reshape(vesicles, 2, LANES)], axis=1)
    rim = tiles[:RIM_VES]
    low = lax.ppermute(rim, "group", forward)
    high = lax.ppermute(rim, "group", backward)

    outgoing = pl.pallas_call(
        pick_kernel,
        out_shape=jax.ShapeDtypeStruct((total_slots, 8, LANES), F32),
        in_specs=[smem(), vmem()],
        out_specs=vmem(),
        name="pick",
    )(asked_for, tiles)
    received = lax.all_to_all(
        outgoing.reshape(members, slots.cap, 8, LANES),
        "member",
        split_axis=0,
        concat_axis=0,
        tiled=True,
    )

    rim_row = (
        total_slots
        + jnp.where(owner_group < group_here, 0, RIM_VES)
        + jnp.minimum(owner_slot, RIM_VES - 1)
    )
    end_row = jnp.where(inside, end_slot, jnp.where(end_live, rim_row, 0))
    live_pairs = jnp.sum((pair_list[:, 0] >= 0).astype(jnp.int32))
    meta = jnp.concatenate([end_row, live_pairs[None]]).astype(jnp.int32)
    offsets = jnp.concatenate([pair_offset.T, -pair_offset.T], axis=1).reshape(-1, 1)

    lat, lon, weights = factor_tables()
    rows = 264
    slot_force, low_force, high_force = pl.pallas_call(
        functools.partial(pair_kernel, slots, rows),
        out_shape=(
            jax.ShapeDtypeStruct((total_slots * 8, LANES), F32),
            jax.ShapeDtypeStruct((RIM_VES * 8, LANES), F32),
            jax.ShapeDtypeStruct((RIM_VES * 8, LANES), F32),
        ),
        in_specs=[smem()] + [vmem()] * 7,
        out_specs=(vmem(),) * 3,
        scratch_shapes=[
            pltpu.VMEM(((total_slots + 2 * RIM_VES) * 8, LANES), F32),
            pltpu.VMEM((2 * pairs * 8, LANES), F32),
            pltpu.VMEM((3 * LANES, PADDED), F32),
            pltpu.VMEM((6 * pairs, PADDED), F32),
            pltpu.VMEM((6 * pairs, PADDED), F32),
            pltpu.VMEM((PADDED, LANES), F32),
            pltpu.VMEM((TILES, pairs * FEATURES, LANES), F32),
            pltpu.VMEM((pairs // 2, PADDED, LANES), F32),
            pltpu.VMEM((TILES, pairs * FEATURES, LANES), F32),
            pltpu.VMEM((2 * FEATURES, PADDED), BF16),
            pltpu.VMEM((3, 8, PADDED), F32),
            pltpu.VMEM((3, 8, PADDED), F32),
            pltpu.VMEM((3, rows // 8, 8, LANES), F32),
            pltpu.VMEM((3, rows // 8, 8, LANES), F32),
        ],
        compiler_params=pltpu.CompilerParams(vmem_limit_bytes=56 << 20),
        name="pair_forces",
    )(
        meta,
        offsets,
        jnp.asarray(lat),
        jnp.asarray(lon),
        jnp.asarray(weights),
        received.reshape(total_slots * 8, LANES),
        low.reshape(RIM_VES * 8, LANES),
        high.reshape(RIM_VES * 8, LANES),
    )
    returned = lax.all_to_all(
        slot_force.reshape(members, slots.cap, 8, LANES),
        "member",
        split_axis=0,
        concat_axis=0,
        tiled=True,
    )
    from_low = lax.ppermute(high_force.reshape(RIM_VES, 8, LANES), "group", forward)
    from_high = lax.ppermute(low_force.reshape(RIM_VES, 8, LANES), "group", backward)
    return pl.pallas_call(
        collect_kernel,
        out_shape=jax.ShapeDtypeStruct(coefficients.shape, F32),
        in_specs=[smem()] + [vmem()] * 3,
        out_specs=vmem(),
        scratch_shapes=[pltpu.VMEM((vesicles + 1, 8, LANES), F32)],
        name="collect",
    )(asked_for, returned.reshape(total_slots, 8, LANES), from_low, from_high)


def solution(mesh):
    return jax.shard_map(
        per_device,
        mesh=mesh,
        in_specs=(
            P(("group", "member"), None, None),
            P(("group", "member"), None),
            P(("group", "member"), None),
        ),
        out_specs=P(("group", "member"), None, None),
        check_vma=False,
    )
```
